32 devices in a mesh: grp: 2 (over y), gx: 16 (over z, x, core).
Axes of the slice: x: 2, y: 2, z: 4, core: 2. Of those that a mesh axis runs over, the one named last changes fastest.
Arguments:
- mesh_feature_array: bfloat16 [128, 32, 32, 512], P(('grp', 'gx')), parts along dimension 0, may hold values from -6 to 6
- stencil_coefficients: float32 [27, 512], replicated, may hold values from -1.25 to 1.25
- partition_affinity_matrix: bfloat16 [512, 512], replicated, may hold values from -16 to 16
- softness_mapping_matrix: float32 [512], replicated, may hold values from -0.25 to 0.25
- content_mapping_matrix: bfloat16 [512, 512], replicated, may hold values from -0.25 to 0.25
- layernorm_multiplier: float32 [512], replicated, may hold values from 0.1 to 1.9
- widening_matrix: bfloat16 [512, 1024], replicated, may hold values from -0.25 to 0.25
- narrowing_matrix: bfloat16 [1024, 512], replicated, may hold values from -0.1875 to 0.1875
- final_mapping_matrix: bfloat16 [512, 512], replicated, may hold values from -0.25 to 0.25
Outputs:
- updated: bfloat16 [128, 32, 32, 512], P(('grp', 'gx')), parts along dimension 0
- slice_out: bfloat16 [1024, 512], P(('grp', 'gx')), parts along dimension 0
The draws below stay inside these ranges and needn't reach their ends.
There are 2 independent parts, one for each index of `grp`. The reference program is written for one: setup_inputs(seed, part) draws one part's arguments, and reference() takes and returns one part's arrays. A program takes and returns all parts, laid end to end along the dimension named above; an argument that names none is the same for every part. Nothing has to cross between parts.
All inputs are finite; a program needn't handle non-finite values.
Results may differ from the reference program's by a relative error of at most 0.0056.
Values may be sent and summed in bfloat16 or wider, within the bound.
A program may use at most 128 MiB of HBM per device.

```python
import math
import jax
import jax.numpy as jnp
from jax import lax

CHANNEL_COUNT = 512
M = 512
HID = 1024
NY = 32
NZ = 32
NX = 64


def draw_partition_affinity_matrix(key, part):
    key = jax.random.fold_in(key, 7)
    key_base = jax.random.fold_in(key, 0)
    base = jax.random.normal(key_base, (CHANNEL_COUNT, M), jnp.float32) * (3.0 / math.sqrt(CHANNEL_COUNT))
    return jnp.clip(base, -16.0, 16.0).astype(jnp.bfloat16)


def block_scale(rng, shape, cuts, low, top_value):
    loudness = 1.0
    for dim, blocks in cuts:
        steps = jax.random.uniform(jax.random.fold_in(jax.random.fold_in(rng, 6), dim), (blocks,), jnp.float32, low / len(cuts), top_value / len(cuts))
        loudness = loudness * jnp.repeat(jnp.exp(steps), shape[dim] // blocks).reshape((-1,) + (1,) * (len(shape) - 1 - dim))
    return loudness


def gaussian(rng, dims, width, most, pieces=(), dtype=jnp.bfloat16):
    loudness = block_scale(rng, dims, pieces, -0.22, 0.18) if pieces else 1.0
    drawn = jax.random.normal(rng, dims, jnp.float32) * width * loudness
    return jnp.minimum(jnp.maximum(drawn, -most), most).astype(dtype)


def setup_inputs(seed: int = 0, part: int = 0) -> dict:
    arg_keys = jax.random.split(jax.random.key(seed), 10)
    part_splits = jax.random.split(jax.random.fold_in(arg_keys[9], part), 10)
    mesh_feature_array = gaussian(part_splits[0], (NX, NY, NZ, CHANNEL_COUNT), 1.0, 6.0, ((0, 16),))
    stencil_coefficients = gaussian(arg_keys[1], (27, CHANNEL_COUNT), 27 ** -0.5, 1.25, (), jnp.float32)
    partition_affinity_matrix = draw_partition_affinity_matrix(jax.random.fold_in(arg_keys[9], 71), part)
    softness_mapping_matrix = gaussian(arg_keys[3], (CHANNEL_COUNT,), CHANNEL_COUNT ** -0.5, 0.25, (), jnp.float32)
    content_mapping_matrix = gaussian(arg_keys[4], (CHANNEL_COUNT, CHANNEL_COUNT), CHANNEL_COUNT ** -0.5, 0.25)
    layernorm_multiplier = jnp.clip(1.0 + 0.18 * jax.random.normal(arg_keys[5], (CHANNEL_COUNT,), jnp.float32), 0.1, 1.9)
    widening_matrix = gaussian(arg_keys[6], (CHANNEL_COUNT, HID), CHANNEL_COUNT ** -0.5, 0.25)
    narrowing_matrix = gaussian(arg_keys[7], (HID, CHANNEL_COUNT), HID ** -0.5, 0.1875)
    final_mapping_matrix = gaussian(arg_keys[8], (CHANNEL_COUNT, CHANNEL_COUNT), CHANNEL_COUNT ** -0.5, 0.25)
    return {"mesh_feature_array": mesh_feature_array, "stencil_coefficients": stencil_coefficients, "partition_affinity_matrix": partition_affinity_matrix, "softness_mapping_matrix": softness_mapping_matrix, "content_mapping_matrix": content_mapping_matrix, "layernorm_multiplier": layernorm_multiplier, "widening_matrix": widening_matrix, "narrowing_matrix": narrowing_matrix, "final_mapping_matrix": final_mapping_matrix}


epsilon = 1e-05

def conv_gelu(padded, stencil_coefficients, size_x, size_y, size_z):
    total = jnp.zeros((size_x, size_y, size_z, stencil_coefficients.shape[1]), jnp.float32)
    for offset_a in range(3):
        for offset_b in range(3):
            for offset_c in range(3):
                window = padded[offset_a:offset_a + size_x, offset_b:offset_b + size_y, offset_c:offset_c + size_z]
                total = total + window.astype(jnp.float32) * stencil_coefficients[9 * offset_a + 3 * offset_b + offset_c]
    return jax.nn.gelu(total).astype(jnp.bfloat16)

def owner_mlp(tokens, layernorm_multiplier, widening_matrix, narrowing_matrix):
    center = lax.optimization_barrier(jnp.mean(tokens, axis=-1, keepdims=True))
    spread = lax.optimization_barrier(jnp.mean((tokens - center) ** 2, axis=-1, keepdims=True))
    normed = ((tokens - center) * lax_rsqrt(spread + epsilon) * layernorm_multiplier).astype(jnp.bfloat16)
    inner = jax.nn.gelu(jnp.dot(normed, widening_matrix, preferred_element_type=jnp.float32)).astype(jnp.bfloat16)
    return (tokens + jnp.dot(inner, narrowing_matrix, preferred_element_type=jnp.float32)).astype(jnp.bfloat16)

def lax_rsqrt(value):
    return 1.0 / jnp.sqrt(value)

def reference(mesh_feature_array, stencil_coefficients, partition_affinity_matrix, softness_mapping_matrix, content_mapping_matrix, layernorm_multiplier, widening_matrix, narrowing_matrix, final_mapping_matrix):
    padded = jnp.pad(mesh_feature_array, ((1, 1), (1, 1), (1, 1), (0, 0)))
    intermediate_response = conv_gelu(padded, stencil_coefficients, NX, NY, NZ).reshape(-1, CHANNEL_COUNT)
    local_softness_factor = 0.25 + jax.nn.softplus(jnp.dot(intermediate_response, softness_mapping_matrix.astype(jnp.bfloat16), preferred_element_type=jnp.float32))
    partition_affinity_raw = jnp.dot(intermediate_response, partition_affinity_matrix, preferred_element_type=jnp.float32) / local_softness_factor[:, None]
    slice_probs = jax.nn.softmax(partition_affinity_raw, axis=-1).astype(jnp.bfloat16)
    values = jnp.dot(intermediate_response, content_mapping_matrix, preferred_element_type=jnp.float32).astype(jnp.bfloat16)
    weighted_tokens = jax.lax.dot_general(slice_probs, values, (((0,), (0,)), ((), ())), preferred_element_type=jnp.float32)
    mass = lax.optimization_barrier(jnp.sum(slice_probs.astype(jnp.float32), axis=0))
    tokens = weighted_tokens / (mass[:, None] + epsilon)
    slice_out = owner_mlp(tokens, layernorm_multiplier, widening_matrix, narrowing_matrix)
    desliced = jnp.dot(slice_probs, slice_out, preferred_element_type=jnp.float32).astype(jnp.bfloat16)
    flat = mesh_feature_array.reshape(-1, CHANNEL_COUNT).astype(jnp.float32)
    updated = (flat + jnp.dot(desliced, final_mapping_matrix, preferred_element_type=jnp.float32)).astype(jnp.bfloat16)
    return (updated.reshape(NX, NY, NZ, CHANNEL_COUNT), slice_out)
```

```python
import functools
import math

import jax
import jax.numpy as jnp
from jax import lax
from jax.experimental import pallas as pl
from jax.experimental.pallas import tpu as pltpu
from jax.sharding import PartitionSpec as P

epsilon = 1e-05
MESH = pl.DeviceIdType.MESH
F32 = jnp.float32
BF16 = jnp.bfloat16
LANES = 128
VMEM_LIMIT = 60 * 1024 * 1024


def gelu(v):
    a = math.sqrt(2.0 / math.pi)
    return 0.5 * v * (1.0 + jnp.tanh(v * (a + (a * 0.044715) * (v * v))))


def slab_kernel(
    plan, first, count, n_src, has_prior, last, rows_per_step, *refs
):
    refs = list(refs)
    srcs = [refs.pop(0) for _ in range(n_src)]
    taps_ref, aff_ref, soft_ref = (refs.pop(0) for _ in range(3))
    g_in = None
    if has_prior:
        refs.pop(0)
        g_in = refs.pop(0)
    p_out, g_out, pad, hid, prob, load_sem, store_sem = refs
    planes_in, rows_y2, rows_z, channels = pad.shape
    rows_y = rows_y2 - 2
    cells = rows_y * rows_z
    slices = aff_ref.shape[1]

    loads = []
    for i, (s, j) in enumerate(plan):
        copy = pltpu.make_async_copy(
            srcs[s].at[j], pad.at[i, pl.ds(1, rows_y)], load_sem.at[i]
        )
        copy.start()
        loads.append(copy)
    for i in range(planes_in):
        pad[i, 0] = jnp.zeros((rows_z, channels), BF16)
        pad[i, rows_y + 1] = jnp.zeros((rows_z, channels), BF16)
    for copy in loads:
        copy.wait()

    row = lax.broadcasted_iota(jnp.int32, (rows_z, LANES), 0)
    ones = jnp.ones((cells, LANES), BF16)
    stores = []
    for k in range(count):

        def conv_row(y, carry):
            for ch in range(channels // LANES):
                cs = pl.ds(ch * LANES, LANES)
                sums = [None, None, None]
                for a in range(3):
                    parts = [None, None, None]
                    for b in range(3):
                        v = pad[k + a, y + b, :, cs].reshape(rows_z // 16, 16, LANES)
                        for c in range(3):
                            t = v * taps_ref[9 * a + 3 * b + c, :, cs]
                            parts[c] = t if parts[c] is None else parts[c] + t
                    for c in range(3):
                        t = parts[c].astype(F32)
                        sums[c] = t if sums[c] is None else sums[c] + t
                s0, s1, s2 = (t.reshape(rows_z, LANES) for t in sums)
                total = (
                    s1
                    + jnp.where(row == 0, 0.0, pltpu.roll(s0, 1, 0))
                    + jnp.where(row == rows_z - 1, 0.0, pltpu.roll(s2, rows_z - 1, 0))
                )
                hid[pl.ds(pl.multiple_of(y * rows_z, rows_z), rows_z), cs] = gelu(
                    total
                ).astype(BF16)
            return carry

        lax.fori_loop(0, rows_y, conv_row, 0)

        def soft_step(i, carry):
            rs = pl.ds(pl.multiple_of(i * rows_per_step, rows_per_step), rows_per_step)
            h = hid[rs, :]
            logits = jnp.dot(h, aff_ref[...], preferred_element_type=F32)
            z = jnp.dot(h, soft_ref[...], preferred_element_type=F32)
            temp = 0.25 + jnp.maximum(z, 0.0) + jnp.log1p(jnp.exp(-jnp.abs(z)))
            scale = (1.0 / temp)[:, :1]
            top = jnp.max(logits, axis=-1, keepdims=True)
            e = jnp.exp((logits - top) * scale)
            e = e * (1.0 / jnp.sum(e, axis=-1, keepdims=True))
            prob[k, rs, :] = e.astype(BF16)
            return carry

        lax.fori_loop(0, cells // rows_per_step, soft_step, 0)
        store = pltpu.make_async_copy(prob.at[k], p_out.at[first + k], store_sem.at[k])
        store.start()
        stores.append(store)
        contract = (((0,), (0,)), ((), ()))
        pk = prob[k]
        g = lax.dot_general(pk, hid[...], contract, preferred_element_type=F32)
        m = lax.dot_general(pk, ones, contract, preferred_element_type=F32)
        if k == 0:
            if has_prior:
                g = g + g_in[:, :channels]
                m = m + g_in[:, channels:]
        else:
            g = g + acc_g
            m = m + acc_m
        acc_g, acc_m = g, m
    if last:
        g_out[:, :channels] = acc_g.astype(BF16)
        high = acc_m.astype(BF16).astype(F32)
        lane = lax.broadcasted_iota(jnp.int32, (slices, LANES), 1)
        g_out[:, channels:] = jnp.where(lane < LANES // 2, high, acc_m - high).astype(BF16)
    else:
        g_out[:, :channels] = acc_g
        g_out[:, channels:] = acc_m
    for store in stores:
        store.wait()


def slab(plan, first, srcs, planes, taps, aff, soft, prior, last):
    _, rows_y, rows_z, channels = srcs[0].shape
    slices = aff.shape[1]
    count = len(plan) - 2
    cells = rows_y * rows_z
    any_spec = pl.BlockSpec(memory_space=pl.ANY)
    vmem_spec = pl.BlockSpec(memory_space=pltpu.VMEM)
    args = list(srcs) + [taps, aff, soft]
    specs = [any_spec] * len(srcs) + [vmem_spec] * 3
    aliases = {}
    if prior is not None:
        aliases = {len(args): 0}
        args += list(prior)
        specs += [any_spec, vmem_spec]
    return pl.pallas_call(
        functools.partial(
            slab_kernel, plan, first, count, len(srcs), prior is not None, last, min(128, cells)
        ),
        out_shape=(
            jax.ShapeDtypeStruct((planes, cells, slices), BF16),
            jax.ShapeDtypeStruct((slices, channels + LANES), BF16 if last else F32),
        ),
        in_specs=specs,
        out_specs=(any_spec, vmem_spec),
        input_output_aliases=aliases,
        scratch_shapes=[
            pltpu.VMEM((count + 2, rows_y + 2, rows_z, channels), BF16),
            pltpu.VMEM((cells, channels), BF16),
            pltpu.VMEM((count, cells, slices), BF16),
            pltpu.SemaphoreType.DMA((count + 2,)),
            pltpu.SemaphoreType.DMA((count,)),
        ],
        compiler_params=pltpu.CompilerParams(vmem_limit_bytes=VMEM_LIMIT),
        cost_estimate=pl.CostEstimate(
            flops=count * cells * (4 * channels * slices + 200 * channels),
            bytes_accessed=count * cells * channels * 6,
            transcendentals=2 * count * cells * channels,
        ),
        name="slab_last" if last else ("slab_next" if prior is not None else "slab_first"),
    )(*args)


def exchange_kernel(
    n,
    g_ref,
    gain_ref,
    wc_hbm,
    w1_hbm,
    w2_hbm,
    wf_hbm,
    own_ref,
    all_ref,
    wc,
    w1,
    w2,
    wf,
    pair_in,
    summed,
    ring_in,
    w_sem,
    s1,
    r1,
    s2,
    r2,
    s3,
    r3,
    s4,
    r4,
):
    me = lax.axis_index("gx")
    half = n // 2
    core = lax.rem(me, 2)
    chip = me // 2
    partner = me + 1 - 2 * core
    channels = wc.shape[0]

    def there(d):
        return 2 * lax.rem(chip + d, half) + core

    def origin(d):
        return lax.rem(chip + half - d, half)

    loads = []
    for i, (src, dst) in enumerate(((wc_hbm, wc), (w1_hbm, w1), (w2_hbm, w2), (wf_hbm, wf))):
        copy = pltpu.make_async_copy(src, dst, w_sem.at[i])
        copy.start()
        loads.append(copy)

    barrier = pltpu.get_barrier_semaphore()
    pl.semaphore_signal(barrier, inc=1, device_id={"gx": partner}, device_id_type=MESH)
    for d in range(1, half):
        pl.semaphore_signal(barrier, inc=1, device_id={"gx": there(d)}, device_id_type=MESH)
    pl.semaphore_wait(barrier, half)

    def remote(src, dst, ss, rs, to):
        return pltpu.make_async_remote_copy(
            src_ref=src, dst_ref=dst, send_sem=ss, recv_sem=rs,
            device_id={"gx": to}, device_id_type=MESH,
        )

    pair = []
    for d in range(half):
        k = lax.rem(chip + (d + 1) % half, half)
        copy = remote(g_ref.at[k, 1 - core], pair_in.at[k], s1.at[d], r1.at[d], partner)
        copy.start()
        pair.append(copy)
    sends = []
    for d in range(1, half):
        k = lax.rem(chip + d, half)
        pair[d - 1].wait_recv()
        summed[k] = (g_ref[k, core].astype(F32) + pair_in[k].astype(F32)).astype(BF16)
        copy = remote(summed.at[k], ring_in.at[d], s2.at[d], r2.at[d], there(d))
        copy.start()
        sends.append(copy)
    pair[half - 1].wait_recv()
    acc = g_ref[chip, core].astype(F32) + pair_in[chip].astype(F32)
    for d in range(1, half):
        sends[d - 1].wait_recv()
        acc = acc + ring_in[d].astype(F32)
    for copy in loads:
        copy.wait()

    mass = acc[:, channels : channels + 1] + acc[
        :, channels + LANES // 2 : channels + LANES // 2 + 1
    ]
    mean_hidden = acc[:, :channels] / (mass + epsilon)
    high = mean_hidden.astype(BF16)
    low = (mean_hidden - high.astype(F32)).astype(BF16)
    tokens = jnp.dot(high, wc[...], preferred_element_type=F32) + jnp.dot(
        low, wc[...], preferred_element_type=F32
    )
    center = jnp.mean(tokens, axis=-1, keepdims=True)
    spread = jnp.mean((tokens - center) ** 2, axis=-1, keepdims=True)
    normed = ((tokens - center) * (1.0 / jnp.sqrt(spread + epsilon)) * gain_ref[...]).astype(BF16)
    inner = gelu(jnp.dot(normed, w1[...], preferred_element_type=F32)).astype(BF16)
    own = (tokens + jnp.dot(inner, w2[...], preferred_element_type=F32)).astype(BF16)
    own_ref[...] = own
    all_ref[me] = jnp.dot(own, wf[...], preferred_element_type=F32).astype(BF16)

    out = []
    for d in range(1, half):
        copy = remote(all_ref.at[me], all_ref.at[me], s3.at[d], r3.at[d], there(d))
        copy.start()
        out.append(copy)
    first = remote(all_ref.at[me], all_ref.at[me], s4.at[0], r4.at[0], partner)
    first.start()
    relays = [first]
    for d in range(1, half):
        out[d - 1].wait_recv()
        block = 2 * origin(d) + core
        copy = remote(all_ref.at[block], all_ref.at[block], s4.at[d], r4.at[d], partner)
        copy.start()
        relays.append(copy)
    for copy in pair + sends + out:
        copy.wait_send()
    for copy in relays:
        copy.wait()


def exchange(n, g, gain, wc, w1, w2, wf):
    slices, width = g.shape
    channels = wc.shape[0]
    rows, half = slices // n, n // 2
    any_spec = pl.BlockSpec(memory_space=pl.ANY)
    vmem_spec = pl.BlockSpec(memory_space=pltpu.VMEM)
    dma = pltpu.SemaphoreType.DMA
    return pl.pallas_call(
        functools.partial(exchange_kernel, n),
        out_shape=(
            jax.ShapeDtypeStruct((rows, channels), BF16),
            jax.ShapeDtypeStruct((n, rows, channels), BF16),
        ),
        in_specs=[vmem_spec, vmem_spec] + [any_spec] * 4,
        out_specs=(vmem_spec, vmem_spec),
        scratch_shapes=[
            pltpu.VMEM(wc.shape, BF16),
            pltpu.VMEM(w1.shape, BF16),
            pltpu.VMEM(w2.shape, BF16),
            pltpu.VMEM(wf.shape, BF16),
            pltpu.VMEM((half, rows, width), BF16),
            pltpu.VMEM((half, rows, width), BF16),
            pltpu.VMEM((half, rows, width), BF16),
            dma((4,)),
        ]
        + [dma((half,))] * 8,
        compiler_params=pltpu.CompilerParams(
            collective_id=0, has_side_effects=True, vmem_limit_bytes=VMEM_LIMIT
        ),
        name="exchange",
    )(g.reshape(half, 2, rows, width), gain, wc, w1, w2, wf)


def final_kernel(x_ref, p_ref, f_ref, o_ref):
    o_ref[...] = (
        x_ref[...].astype(F32) + jnp.dot(p_ref[...], f_ref[...], preferred_element_type=F32)
    ).astype(BF16)


def final(x, p, f):
    cells, channels = x.shape
    slices = p.shape[1]
    block = math.gcd(cells, 512)
    return pl.pallas_call(
        final_kernel,
        out_shape=jax.ShapeDtypeStruct((cells, channels), BF16),
        grid=(cells // block,),
        in_specs=[
            pl.BlockSpec((block, channels), lambda i: (i, 0)),
            pl.BlockSpec((block, slices), lambda i: (i, 0)),
            pl.BlockSpec((slices, channels), lambda i: (0, 0)),
        ],
        out_specs=pl.BlockSpec((block, channels), lambda i: (i, 0)),
        compiler_params=pltpu.CompilerParams(vmem_limit_bytes=VMEM_LIMIT),
        name="final",
    )(x, p, f)


def per_device(x, stencil, aff, softness, wc, gain, w1, w2, wf):
    planes, rows_y, rows_z, channels = x.shape
    n = lax.axis_size("gx")
    up = [(i, i + 1) for i in range(n - 1)]
    down = [(j, i) for i, j in up]
    before = lax.ppermute(x[planes - 1 :], "gx", up)
    after = lax.ppermute(x[:1], "gx", down)
    taps = jnp.broadcast_to(stencil.astype(BF16)[:, None, :], (27, 16, channels))
    soft = jnp.broadcast_to(softness.astype(BF16)[:, None], (channels, LANES))
    weights = (taps, aff, soft)
    prior = None
    if planes > 2:
        inside = tuple((0, j) for j in range(planes))
        prior = slab(inside, 1, (x,), planes, *weights, prior, False)
    low = ((1, 0), (0, 0), (0, 1) if planes > 1 else (2, 0))
    prior = slab(low, 0, (x, before, after), planes, *weights, prior, planes == 1)
    if planes > 1:
        high = ((0, planes - 2), (0, planes - 1), (1, 0))
        prior = slab(high, planes - 1, (x, after), planes, *weights, prior, True)
    probs, g = prior
    own, folded = exchange(n, g, gain.reshape(1, -1), wc, w1, w2, wf)
    updated = final(
        x.reshape(-1, channels),
        probs.reshape(planes * rows_y * rows_z, -1),
        folded.reshape(-1, channels),
    )
    return updated.reshape(x.shape), own


def solution(mesh):
    return jax.shard_map(
        per_device,
        mesh=mesh,
        in_specs=(P(("grp", "gx"), None, None, None), P(), P(), P(), P(), P(), P(), P(), P()),
        out_specs=(P(("grp", "gx"), None, None, None), P(("grp", "gx"), None)),
        check_vma=False,
    )
```

```python
import functools
import math

import jax
import jax.numpy as jnp
from jax import lax
from jax.experimental import pallas as pl
from jax.experimental.pallas import tpu as pltpu
from jax.sharding import PartitionSpec as P

epsilon = 1e-05
MESH = pl.DeviceIdType.MESH
F32 = jnp.float32
BF16 = jnp.bfloat16
LANES = 128
MIB = 1024 * 1024
SLAB_LIMIT = 32 * MIB
SMALL_LIMIT = 12 * MIB
CONV_UNROLL = 4
SOFT_UNROLL = 1
STEP_ROWS = 256


def gelu(v):
    a = math.sqrt(2.0 / math.pi)
    return 0.5 * v * (1.0 + jnp.tanh(v * (a + (a * 0.044715) * (v * v))))


def slab_kernel(
    n, step_rows, x_ref, taps_ref, aff_ref, soft_ref, p_out, g_out,
    pad, hid, prob, acc, load_sem, store_sem, send_sem, recv_sem,
):
    planes, rows_y, rows_z, channels = x_ref.shape
    cells = rows_y * rows_z
    slices = aff_ref.shape[1]
    me = lax.axis_index("gx")
    inside = pl.ds(1, rows_y)
    has_left, has_right = me > 0, me < n - 1

    loads = []
    for j in range(planes):
        copy = pltpu.make_async_copy(x_ref.at[j], pad.at[j + 1, inside], load_sem.at[j])
        copy.start()
        loads.append(copy)

    barrier = pltpu.get_barrier_semaphore()

    @pl.when(has_left)
    def _():
        pl.semaphore_signal(barrier, inc=1, device_id={"gx": me - 1}, device_id_type=MESH)

    @pl.when(has_right)
    def _():
        pl.semaphore_signal(barrier, inc=1, device_id={"gx": me + 1}, device_id_type=MESH)

    pl.semaphore_wait(barrier, jnp.minimum(me, 1) + jnp.minimum(n - 1 - me, 1))

    up = pltpu.make_async_remote_copy(
        src_ref=x_ref.at[planes - 1], dst_ref=pad.at[0, inside],
        send_sem=send_sem.at[0], recv_sem=recv_sem.at[0],
        device_id={"gx": me + 1}, device_id_type=MESH,
    )
    down = pltpu.make_async_remote_copy(
        src_ref=x_ref.at[0], dst_ref=pad.at[planes + 1, inside],
        send_sem=send_sem.at[1], recv_sem=recv_sem.at[1],
        device_id={"gx": me - 1}, device_id_type=MESH,
    )

    @pl.when(has_right)
    def _():
        up.start()

    @pl.when(has_left)
    def _():
        down.start()

    for i in range(planes + 2):
        pad[i, 0] = jnp.zeros((rows_z, channels), BF16)
        pad[i, rows_y + 1] = jnp.zeros((rows_z, channels), BF16)

    @pl.when(jnp.logical_not(has_left))
    def _():
        pad[0, inside] = jnp.zeros((rows_y, rows_z, channels), BF16)

    @pl.when(jnp.logical_not(has_right))
    def _():
        pad[planes + 1, inside] = jnp.zeros((rows_y, rows_z, channels), BF16)

    acc[...] = jnp.zeros_like(acc)
    for copy in loads[:3]:
        copy.wait()

    row = lax.broadcasted_iota(jnp.int32, (rows_z, LANES), 0)

    def plane(i, carry):
        @pl.when(i == min(1, planes - 1))
        def _():
            for copy in loads[3:]:
                copy.wait()

        @pl.when(jnp.logical_and(i == max(planes - 2, 0), has_left))
        def _():
            up.wait_recv()

        @pl.when(jnp.logical_and(i == planes - 1, has_right))
        def _():
            down.wait_recv()

        p = jnp.where(i < planes - 2, i + 1, jnp.where(i == planes - 2, 0, planes - 1))

        for ch in range(channels // LANES):
            cs = pl.ds(ch * LANES, LANES)
            taps = [
                jnp.broadcast_to(taps_ref[t, :, cs], (rows_z, LANES)).astype(BF16)
                for t in range(27)
            ]

            def conv_row(y, carry):
                sums = [None, None, None]
                for a in range(3):
                    parts = [None, None, None]
                    for b in range(3):
                        v = pad[p + a, y + b, :, cs]
                        for c in range(3):
                            t = taps[9 * a + 3 * b + c] * v
                            parts[c] = t if parts[c] is None else parts[c] + t
                    for c in range(3):
                        sums[c] = parts[c] if sums[c] is None else sums[c] + parts[c]
                s0, s1, s2 = (t.astype(F32) for t in sums)
                total = (
                    s1
                    + jnp.where(row == 0, 0.0, pltpu.roll(s0, 1, 0))
                    + jnp.where(row == rows_z - 1, 0.0, pltpu.roll(s2, rows_z - 1, 0))
                )
                hid[pl.ds(pl.multiple_of(y * rows_z, rows_z), rows_z), cs] = gelu(
                    total
                ).astype(BF16)
                return carry

            lax.fori_loop(0, rows_y, conv_row, 0, unroll=CONV_UNROLL)

        def soft_step(j, carry):
            rs = pl.ds(pl.multiple_of(j * step_rows, step_rows), step_rows)
            h = hid[rs, :]
            logits = jnp.dot(h, aff_ref[...], preferred_element_type=F32)
            z = jnp.dot(h, soft_ref[...], preferred_element_type=F32)[:, :1]
            temp = 0.25 + jnp.maximum(z, 0.0) + jnp.log1p(jnp.exp(-jnp.abs(z)))
            top = jnp.max(logits, axis=-1, keepdims=True)
            e = jnp.exp((logits - top) * (1.0 / temp))
            prob[p, rs, :] = (e * (1.0 / jnp.sum(e, axis=-1, keepdims=True))).astype(BF16)
            return carry

        lax.fori_loop(0, cells // step_rows, soft_step, 0, unroll=SOFT_UNROLL)
        pltpu.make_async_copy(prob.at[p], p_out.at[p], store_sem.at[p]).start()
        contract = (((0,), (0,)), ((), ()))
        pk = prob[p]
        ones = jnp.ones((cells, LANES), BF16)
        acc[:, :channels] += lax.dot_general(pk, hid[...], contract, preferred_element_type=F32)
        acc[:, channels:] += lax.dot_general(pk, ones, contract, preferred_element_type=F32)
        return carry

    lax.fori_loop(0, planes, plane, 0)
    g_out[:, :channels] = acc[:, :channels].astype(BF16)
    mass = acc[:, channels:]
    high = mass.astype(BF16).astype(F32)
    lane = lax.broadcasted_iota(jnp.int32, (slices, LANES), 1)
    g_out[:, channels:] = jnp.where(lane < LANES // 2, high, mass - high).astype(BF16)
    for j in range(planes):
        pltpu.make_async_copy(prob.at[j], p_out.at[j], store_sem.at[j]).wait()

    @pl.when(has_right)
    def _():
        up.wait_send()

    @pl.when(has_left)
    def _():
        down.wait_send()


def slab(n, x, taps, aff, soft):
    planes, rows_y, rows_z, channels = x.shape
    slices = aff.shape[1]
    cells = rows_y * rows_z
    any_spec = pl.BlockSpec(memory_space=pl.ANY)
    vmem_spec = pl.BlockSpec(memory_space=pltpu.VMEM)
    dma = pltpu.SemaphoreType.DMA
    return pl.pallas_call(
        functools.partial(slab_kernel, n, min(STEP_ROWS, cells)),
        out_shape=(
            jax.ShapeDtypeStruct((planes, cells, slices), BF16),
            jax.ShapeDtypeStruct((slices, channels + LANES), BF16),
        ),
        in_specs=[pl.BlockSpec(memory_space=pltpu.HBM)] + [vmem_spec] * 3,
        out_specs=(any_spec, vmem_spec),
        scratch_shapes=[
            pltpu.VMEM((planes + 2, rows_y + 2, rows_z, channels), BF16),
            pltpu.VMEM((cells, channels), BF16),
            pltpu.VMEM((planes, cells, slices), BF16),
            pltpu.VMEM((slices, channels + LANES), F32),
            dma((planes,)),
            dma((planes,)),
            dma((2,)),
            dma((2,)),
        ],
        compiler_params=pltpu.CompilerParams(
            collective_id=1, has_side_effects=True, vmem_limit_bytes=SLAB_LIMIT
        ),
        name="slab",
    )(x, taps, aff, soft)


def exchange_kernel(
    n,
    g_ref,
    gain_ref,
    wc_hbm,
    w1_hbm,
    w2_hbm,
    wf_hbm,
    own_ref,
    all_ref,
    wc,
    w1,
    w2,
    wf,
    pair_in,
    summed,
    ring_in,
    w_sem,
    s1,
    r1,
    s2,
    r2,
    s3,
    r3,
    s4,
    r4,
):
    me = lax.axis_index("gx")
    half = n // 2
    core = lax.rem(me, 2)
    chip = me // 2
    partner = me + 1 - 2 * core
    channels = wc.shape[0]

    def there(d):
        return 2 * lax.rem(chip + d, half) + core

    def origin(d):
        return lax.rem(chip + half - d, half)

    loads = []
    for i, (src, dst) in enumerate(((wc_hbm, wc), (w1_hbm, w1), (w2_hbm, w2), (wf_hbm, wf))):
        copy = pltpu.make_async_copy(src, dst, w_sem.at[i])
        copy.start()
        loads.append(copy)

    barrier = pltpu.get_barrier_semaphore()
    pl.semaphore_signal(barrier, inc=1, device_id={"gx": partner}, device_id_type=MESH)
    for d in range(1, half):
        pl.semaphore_signal(barrier, inc=1, device_id={"gx": there(d)}, device_id_type=MESH)
    pl.semaphore_wait(barrier, half)

    def remote(src, dst, ss, rs, to):
        return pltpu.make_async_remote_copy(
            src_ref=src, dst_ref=dst, send_sem=ss, recv_sem=rs,
            device_id={"gx": to}, device_id_type=MESH,
        )

    pair = []
    for d in range(half):
        k = lax.rem(chip + (d + 1) % half, half)
        copy = remote(g_ref.at[k, 1 - core], pair_in.at[k], s1.at[d], r1.at[d], partner)
        copy.start()
        pair.append(copy)
    sends = []
    for d in range(1, half):
        k = lax.rem(chip + d, half)
        pair[d - 1].wait_recv()
        summed[k] = (g_ref[k, core].astype(F32) + pair_in[k].astype(F32)).astype(BF16)
        copy = remote(summed.at[k], ring_in.at[d], s2.at[d], r2.at[d], there(d))
        copy.start()
        sends.append(copy)
    pair[half - 1].wait_recv()
    acc = g_ref[chip, core].astype(F32) + pair_in[chip].astype(F32)
    for d in range(1, half):
        sends[d - 1].wait_recv()
        acc = acc + ring_in[d].astype(F32)
    for copy in loads:
        copy.wait()

    mass = acc[:, channels : channels + 1] + acc[
        :, channels + LANES // 2 : channels + LANES // 2 + 1
    ]
    mean_hidden = acc[:, :channels] / (mass + epsilon)
    high = mean_hidden.astype(BF16)
    low = (mean_hidden - high.astype(F32)).astype(BF16)
    tokens = jnp.dot(high, wc[...], preferred_element_type=F32) + jnp.dot(
        low, wc[...], preferred_element_type=F32
    )
    center = jnp.mean(tokens, axis=-1, keepdims=True)
    spread = jnp.mean((tokens - center) ** 2, axis=-1, keepdims=True)
    normed = ((tokens - center) * (1.0 / jnp.sqrt(spread + epsilon)) * gain_ref[...]).astype(BF16)
    inner = gelu(jnp.dot(normed, w1[...], preferred_element_type=F32)).astype(BF16)
    own = (tokens + jnp.dot(inner, w2[...], preferred_element_type=F32)).astype(BF16)
    own_ref[...] = own
    all_ref[me] = jnp.dot(own, wf[...], preferred_element_type=F32).astype(BF16)

    out = []
    for d in range(1, half):
        copy = remote(all_ref.at[me], all_ref.at[me], s3.at[d], r3.at[d], there(d))
        copy.start()
        out.append(copy)
    first = remote(all_ref.at[me], all_ref.at[me], s4.at[0], r4.at[0], partner)
    first.start()
    relays = [first]
    for d in range(1, half):
        out[d - 1].wait_recv()
        block = 2 * origin(d) + core
        copy = remote(all_ref.at[block], all_ref.at[block], s4.at[d], r4.at[d], partner)
        copy.start()
        relays.append(copy)
    for copy in pair + sends + out:
        copy.wait_send()
    for copy in relays:
        copy.wait()


def exchange(n, g, gain, wc, w1, w2, wf):
    slices, width = g.shape
    channels = wc.shape[0]
    rows, half = slices // n, n // 2
    any_spec = pl.BlockSpec(memory_space=pl.ANY)
    vmem_spec = pl.BlockSpec(memory_space=pltpu.VMEM)
    dma = pltpu.SemaphoreType.DMA
    return pl.pallas_call(
        functools.partial(exchange_kernel, n),
        out_shape=(
            jax.ShapeDtypeStruct((rows, channels), BF16),
            jax.ShapeDtypeStruct((n, rows, channels), BF16),
        ),
        in_specs=[vmem_spec, vmem_spec] + [any_spec] * 4,
        out_specs=(vmem_spec, vmem_spec),
        scratch_shapes=[
            pltpu.VMEM(wc.shape, BF16),
            pltpu.VMEM(w1.shape, BF16),
            pltpu.VMEM(w2.shape, BF16),
            pltpu.VMEM(wf.shape, BF16),
            pltpu.VMEM((half, rows, width), BF16),
            pltpu.VMEM((half, rows, width), BF16),
            pltpu.VMEM((half, rows, width), BF16),
            dma((4,)),
        ]
        + [dma((half,))] * 8,
        compiler_params=pltpu.CompilerParams(
            collective_id=0, has_side_effects=True, vmem_limit_bytes=SMALL_LIMIT
        ),
        name="exchange",
    )(g.reshape(half, 2, rows, width), gain, wc, w1, w2, wf)


def final_kernel(x_ref, p_ref, f_ref, o_ref):
    o_ref[...] = (
        x_ref[...].astype(F32) + jnp.dot(p_ref[...], f_ref[...], preferred_element_type=F32)
    ).astype(BF16)


def final(x, p, f):
    cells, channels = x.shape
    slices = p.shape[1]
    block = math.gcd(cells, 512)
    return pl.pallas_call(
        final_kernel,
        out_shape=jax.ShapeDtypeStruct((cells, channels), BF16),
        grid=(cells // block,),
        in_specs=[
            pl.BlockSpec((block, channels), lambda i: (i, 0)),
            pl.BlockSpec((block, slices), lambda i: (i, 0)),
            pl.BlockSpec((slices, channels), lambda i: (0, 0)),
        ],
        out_specs=pl.BlockSpec((block, channels), lambda i: (i, 0)),
        compiler_params=pltpu.CompilerParams(vmem_limit_bytes=SMALL_LIMIT),
        name="final",
    )(x, p, f)


def per_device(x, stencil, aff, softness, wc, gain, w1, w2, wf):
    planes, rows_y, rows_z, channels = x.shape
    n = lax.axis_size("gx")
    soft = jnp.broadcast_to(softness.astype(BF16)[:, None], (channels, LANES))
    probs, g = slab(n, x, stencil[:, None, :], aff, soft)
    own, folded = exchange(n, g, gain.reshape(1, -1), wc, w1, w2, wf)
    updated = final(
        x.reshape(-1, channels),
        probs.reshape(planes * rows_y * rows_z, -1),
        folded.reshape(-1, channels),
    )
    return updated.reshape(x.shape), own


def solution(mesh):
    return jax.shard_map(
        per_device,
        mesh=mesh,
        in_specs=(P(("grp", "gx"), None, None, None), P(), P(), P(), P(), P(), P(), P(), P()),
        out_specs=(P(("grp", "gx"), None, None, None), P(("grp", "gx"), None)),
        check_vma=False,
    )
```

```python
import functools
import math

import jax
import jax.numpy as jnp
from jax import lax
from jax.experimental import pallas as pl
from jax.experimental.pallas import tpu as pltpu
from jax.sharding import PartitionSpec as P

epsilon = 1e-05
MESH = pl.DeviceIdType.MESH
F32 = jnp.float32
BF16 = jnp.bfloat16
LANES = 128
MIB = 1024 * 1024
SLAB_LIMIT = 32 * MIB
SMALL_LIMIT = 12 * MIB
CONV_UNROLL = 4
SOFT_UNROLL = 1
STEP_ROWS = 256


def gelu(v):
    a = math.sqrt(2.0 / math.pi)
    return 0.5 * v * (1.0 + jnp.tanh(v * (a + (a * 0.044715) * (v * v))))


def slab_kernel(
    n, step_rows, x_ref, taps_hbm, aff_hbm, soft_hbm, p_out, g_out,
    taps_ref, aff_ref, soft_ref, pad, hid, prob, acc,
    load_sem, small_sem, store_sem, send_sem, recv_sem,
):
    planes, rows_y, rows_z, channels = x_ref.shape
    cells = rows_y * rows_z
    slices = aff_ref.shape[1]
    me = lax.axis_index("gx")
    inside = pl.ds(1, rows_y)
    has_left, has_right = me > 0, me < n - 1
    core, early = lax.rem(me, 2), max(planes - 2, 0)

    small = []
    for i, (src, dst) in enumerate(
        ((taps_hbm, taps_ref), (aff_hbm, aff_ref), (soft_hbm, soft_ref))
    ):
        copy = pltpu.make_async_copy(src, dst, small_sem.at[i])
        copy.start()
        small.append(copy)
    loads = []
    for j in range(planes):
        copy = pltpu.make_async_copy(x_ref.at[j], pad.at[j + 1, inside], load_sem.at[j])
        copy.start()
        loads.append(copy)

    barrier = pltpu.get_barrier_semaphore()

    @pl.when(has_left)
    def _():
        pl.semaphore_signal(barrier, inc=1, device_id={"gx": me - 1}, device_id_type=MESH)

    @pl.when(has_right)
    def _():
        pl.semaphore_signal(barrier, inc=1, device_id={"gx": me + 1}, device_id_type=MESH)

    pl.semaphore_wait(barrier, jnp.minimum(me, 1) + jnp.minimum(n - 1 - me, 1))

    up = pltpu.make_async_remote_copy(
        src_ref=x_ref.at[planes - 1], dst_ref=pad.at[0, inside],
        send_sem=send_sem.at[0], recv_sem=recv_sem.at[0],
        device_id={"gx": me + 1}, device_id_type=MESH,
    )
    down = pltpu.make_async_remote_copy(
        src_ref=x_ref.at[0], dst_ref=pad.at[planes + 1, inside],
        send_sem=send_sem.at[1], recv_sem=recv_sem.at[1],
        device_id={"gx": me - 1}, device_id_type=MESH,
    )

    @pl.when(has_right)
    def _():
        up.start()

    @pl.when(has_left)
    def _():
        down.start()

    for i in range(planes + 2):
        pad[i, 0] = jnp.zeros((rows_z, channels), BF16)
        pad[i, rows_y + 1] = jnp.zeros((rows_z, channels), BF16)

    @pl.when(jnp.logical_not(has_left))
    def _():
        pad[0, inside] = jnp.zeros((rows_y, rows_z, channels), BF16)

    @pl.when(jnp.logical_not(has_right))
    def _():
        pad[planes + 1, inside] = jnp.zeros((rows_y, rows_z, channels), BF16)

    acc[...] = jnp.zeros_like(acc)
    for copy in loads[:3] + small:
        copy.wait()

    row = lax.broadcasted_iota(jnp.int32, (rows_z, LANES), 0)
    soft = jnp.broadcast_to(soft_ref[...].astype(BF16), (LANES, channels))

    def plane(i, carry):
        @pl.when(i == min(1, planes - 1))
        def _():
            for copy in loads[3:]:
                copy.wait()

        @pl.when(jnp.logical_and(i == jnp.where(core == 0, planes - 1, early), has_left))
        def _():
            up.wait_recv()

        @pl.when(jnp.logical_and(i == jnp.where(core == 0, early, planes - 1), has_right))
        def _():
            down.wait_recv()

        p = jnp.where(i < planes - 2, i + 1, jnp.where((i == planes - 1) == (core == 0), 0, planes - 1))

        for ch in range(channels // LANES):
            cs = pl.ds(ch * LANES, LANES)
            taps = [
                jnp.broadcast_to(taps_ref[t : t + 1, cs], (rows_z, LANES)).astype(BF16)
                for t in range(27)
            ]

            def conv_row(y, carry):
                sums = [None, None, None]
                for a in range(3):
                    parts = [None, None, None]
                    for b in range(3):
                        v = pad[p + a, y + b, :, cs]
                        for c in range(3):
                            t = taps[9 * a + 3 * b + c] * v
                            parts[c] = t if parts[c] is None else parts[c] + t
                    for c in range(3):
                        sums[c] = parts[c] if sums[c] is None else sums[c] + parts[c]
                s0, s1, s2 = (t.astype(F32) for t in sums)
                total = (
                    s1
                    + jnp.where(row == 0, 0.0, pltpu.roll(s0, 1, 0))
                    + jnp.where(row == rows_z - 1, 0.0, pltpu.roll(s2, rows_z - 1, 0))
                )
                hid[pl.ds(pl.multiple_of(y * rows_z, rows_z), rows_z), cs] = gelu(
                    total
                ).astype(BF16)
                return carry

            lax.fori_loop(0, rows_y, conv_row, 0, unroll=CONV_UNROLL)

        def soft_step(j, carry):
            rs = pl.ds(pl.multiple_of(j * step_rows, step_rows), step_rows)
            h = hid[rs, :]
            logits = jnp.dot(h, aff_ref[...], preferred_element_type=F32)
            z = lax.dot_general(h, soft, (((1,), (1,)), ((), ())), preferred_element_type=F32)[:, :1]
            temp = 0.25 + jnp.maximum(z, 0.0) + jnp.log1p(jnp.exp(-jnp.abs(z)))
            top = jnp.max(logits, axis=-1, keepdims=True)
            e = jnp.exp((logits - top) * (1.0 / temp))
            prob[p, rs, :] = (e * (1.0 / jnp.sum(e, axis=-1, keepdims=True))).astype(BF16)
            return carry

        lax.fori_loop(0, cells // step_rows, soft_step, 0, unroll=SOFT_UNROLL)
        pltpu.make_async_copy(prob.at[p], p_out.at[p], store_sem.at[p]).start()
        contract = (((0,), (0,)), ((), ()))
        pk = prob[p]
        ones = jnp.ones((cells, LANES), BF16)
        acc[:, :channels] += lax.dot_general(pk, hid[...], contract, preferred_element_type=F32)
        acc[:, channels:] += lax.dot_general(pk, ones, contract, preferred_element_type=F32)
        return carry

    lax.fori_loop(0, planes, plane, 0)
    g_out[:, :channels] = acc[:, :channels].astype(BF16)
    mass = acc[:, channels:]
    high = mass.astype(BF16).astype(F32)
    lane = lax.broadcasted_iota(jnp.int32, (slices, LANES), 1)
    g_out[:, channels:] = jnp.where(lane < LANES // 2, high, mass - high).astype(BF16)
    for j in range(planes):
        pltpu.make_async_copy(prob.at[j], p_out.at[j], store_sem.at[j]).wait()

    @pl.when(has_right)
    def _():
        up.wait_send()

    @pl.when(has_left)
    def _():
        down.wait_send()


def slab(n, x, taps, aff, soft):
    planes, rows_y, rows_z, channels = x.shape
    slices = aff.shape[1]
    cells = rows_y * rows_z
    any_spec = pl.BlockSpec(memory_space=pl.ANY)
    vmem_spec = pl.BlockSpec(memory_space=pltpu.VMEM)
    dma = pltpu.SemaphoreType.DMA
    return pl.pallas_call(
        functools.partial(slab_kernel, n, min(STEP_ROWS, cells)),
        out_shape=(
            jax.ShapeDtypeStruct((planes, cells, slices), BF16),
            jax.ShapeDtypeStruct((slices, channels + LANES), BF16),
        ),
        in_specs=[pl.BlockSpec(memory_space=pltpu.HBM)] * 4,
        out_specs=(any_spec, vmem_spec),
        scratch_shapes=[
            pltpu.VMEM(taps.shape, F32),
            pltpu.VMEM(aff.shape, BF16),
            pltpu.VMEM(soft.shape, F32),
            pltpu.VMEM((planes + 2, rows_y + 2, rows_z, channels), BF16),
            pltpu.VMEM((cells, channels), BF16),
            pltpu.VMEM((planes, cells, slices), BF16),
            pltpu.VMEM((slices, channels + LANES), F32),
            dma((planes,)),
            dma((3,)),
            dma((planes,)),
            dma((2,)),
            dma((2,)),
        ],
        compiler_params=pltpu.CompilerParams(
            collective_id=1, has_side_effects=True, vmem_limit_bytes=SLAB_LIMIT
        ),
        name="slab",
    )(x, taps, aff, soft)


def exchange_kernel(
    n,
    g_ref,
    gain_hbm,
    wc_hbm,
    w1_hbm,
    w2_hbm,
    wf_hbm,
    own_ref,
    all_ref,
    gain_ref,
    wc,
    w1,
    w2,
    wf,
    pair_in,
    summed,
    ring_in,
    w_sem,
    s1,
    r1,
    s2,
    r2,
    s3,
    r3,
    s4,
    r4,
):
    me = lax.axis_index("gx")
    half = n // 2
    core = lax.rem(me, 2)
    chip = me // 2
    partner = me + 1 - 2 * core
    channels = wc.shape[0]

    def there(d):
        return 2 * lax.rem(chip + d, half) + core

    def origin(d):
        return lax.rem(chip + half - d, half)

    loads = []
    for i, (src, dst) in enumerate(
        ((wc_hbm, wc), (w1_hbm, w1), (w2_hbm, w2), (wf_hbm, wf), (gain_hbm, gain_ref))
    ):
        copy = pltpu.make_async_copy(src, dst, w_sem.at[i])
        copy.start()
        loads.append(copy)

    barrier = pltpu.get_barrier_semaphore()
    pl.semaphore_signal(barrier, inc=1, device_id={"gx": partner}, device_id_type=MESH)
    for d in range(1, half):
        pl.semaphore_signal(barrier, inc=1, device_id={"gx": there(d)}, device_id_type=MESH)
    pl.semaphore_wait(barrier, half)

    def remote(src, dst, ss, rs, to):
        return pltpu.make_async_remote_copy(
            src_ref=src, dst_ref=dst, send_sem=ss, recv_sem=rs,
            device_id={"gx": to}, device_id_type=MESH,
        )

    pair = []
    for d in range(half):
        k = lax.rem(chip + (d + 1) % half, half)
        copy = remote(g_ref.at[k, 1 - core], pair_in.at[k], s1.at[d], r1.at[d], partner)
        copy.start()
        pair.append(copy)
    sends = []
    for d in range(1, half):
        k = lax.rem(chip + d, half)
        pair[d - 1].wait_recv()
        summed[k] = (g_ref[k, core].astype(F32) + pair_in[k].astype(F32)).astype(BF16)
        copy = remote(summed.at[k], ring_in.at[d], s2.at[d], r2.at[d], there(d))
        copy.start()
        sends.append(copy)
    pair[half - 1].wait_recv()
    acc = g_ref[chip, core].astype(F32) + pair_in[chip].astype(F32)
    for d in range(1, half):
        sends[d - 1].wait_recv()
        acc = acc + ring_in[d].astype(F32)
    for copy in loads:
        copy.wait()

    mass = acc[:, channels : channels + 1] + acc[
        :, channels + LANES // 2 : channels + LANES // 2 + 1
    ]
    mean_hidden = acc[:, :channels] / (mass + epsilon)
    high = mean_hidden.astype(BF16)
    low = (mean_hidden - high.astype(F32)).astype(BF16)
    tokens = jnp.dot(high, wc[...], preferred_element_type=F32) + jnp.dot(
        low, wc[...], preferred_element_type=F32
    )
    center = jnp.mean(tokens, axis=-1, keepdims=True)
    spread = jnp.mean((tokens - center) ** 2, axis=-1, keepdims=True)
    normed = ((tokens - center) * (1.0 / jnp.sqrt(spread + epsilon)) * gain_ref[...]).astype(BF16)
    inner = gelu(jnp.dot(normed, w1[...], preferred_element_type=F32)).astype(BF16)
    own = (tokens + jnp.dot(inner, w2[...], preferred_element_type=F32)).astype(BF16)
    own_ref[...] = own
    all_ref[me] = jnp.dot(own, wf[...], preferred_element_type=F32).astype(BF16)

    out = []
    for d in range(1, half):
        copy = remote(all_ref.at[me], all_ref.at[me], s3.at[d], r3.at[d], there(d))
        copy.start()
        out.append(copy)
    first = remote(all_ref.at[me], all_ref.at[me], s4.at[0], r4.at[0], partner)
    first.start()
    relays = [first]
    for d in range(1, half):
        out[d - 1].wait_recv()
        block = 2 * origin(d) + core
        copy = remote(all_ref.at[block], all_ref.at[block], s4.at[d], r4.at[d], partner)
        copy.start()
        relays.append(copy)
    for copy in pair + sends + out:
        copy.wait_send()
    for copy in relays:
        copy.wait()


def exchange(n, g, gain, wc, w1, w2, wf):
    slices, width = g.shape
    channels = wc.shape[0]
    rows, half = slices // n, n // 2
    vmem_spec = pl.BlockSpec(memory_space=pltpu.VMEM)
    dma = pltpu.SemaphoreType.DMA
    return pl.pallas_call(
        functools.partial(exchange_kernel, n),
        out_shape=(
            jax.ShapeDtypeStruct((rows, channels), BF16),
            jax.ShapeDtypeStruct((n, rows, channels), BF16),
        ),
        in_specs=[vmem_spec] + [pl.BlockSpec(memory_space=pltpu.HBM)] * 5,
        out_specs=(vmem_spec, vmem_spec),
        scratch_shapes=[
            pltpu.VMEM(gain.shape, F32),
            pltpu.VMEM(wc.shape, BF16),
            pltpu.VMEM(w1.shape, BF16),
            pltpu.VMEM(w2.shape, BF16),
            pltpu.VMEM(wf.shape, BF16),
            pltpu.VMEM((half, rows, width), BF16),
            pltpu.VMEM((half, rows, width), BF16),
            pltpu.VMEM((half, rows, width), BF16),
            dma((5,)),
        ]
        + [dma((half,))] * 8,
        compiler_params=pltpu.CompilerParams(
            collective_id=0, has_side_effects=True, vmem_limit_bytes=SMALL_LIMIT
        ),
        name="exchange",
    )(g.reshape(half, 2, rows, width), gain, wc, w1, w2, wf)


def final_kernel(x_ref, p_ref, f_ref, own_ref, o_ref, own_out):
    own_out[...] = own_ref[...]
    o_ref[...] = (
        x_ref[...].astype(F32) + jnp.dot(p_ref[...], f_ref[...], preferred_element_type=F32)
    ).astype(BF16)


def final(x, p, f, own):
    cells, channels = x.shape
    slices = p.shape[1]
    block = math.gcd(cells, 512)
    return pl.pallas_call(
        final_kernel,
        out_shape=(
            jax.ShapeDtypeStruct((cells, channels), BF16),
            jax.ShapeDtypeStruct(own.shape, BF16),
        ),
        grid=(cells // block,),
        in_specs=[
            pl.BlockSpec((block, channels), lambda i: (i, 0)),
            pl.BlockSpec((block, slices), lambda i: (i, 0)),
            pl.BlockSpec((slices, channels), lambda i: (0, 0)),
            pl.BlockSpec(own.shape, lambda i: (0, 0)),
        ],
        out_specs=(
            pl.BlockSpec((block, channels), lambda i: (i, 0)),
            pl.BlockSpec(own.shape, lambda i: (0, 0)),
        ),
        compiler_params=pltpu.CompilerParams(vmem_limit_bytes=SMALL_LIMIT),
        name="final",
    )(x, p, f, own)


def per_device(x, stencil, aff, softness, wc, gain, w1, w2, wf):
    planes, rows_y, rows_z, channels = x.shape
    n = lax.axis_size("gx")
    def held(v):
        return pltpu.with_memory_space_constraint(v, pltpu.HBM)

    probs, g = slab(n, held(x), held(stencil), held(aff), held(softness.reshape(1, -1)))
    own, folded = exchange(
        n, g, held(gain.reshape(1, -1)), held(wc), held(w1), held(w2), held(wf)
    )
    updated, own = final(
        x.reshape(-1, channels),
        probs.reshape(planes * rows_y * rows_z, -1),
        folded.reshape(-1, channels),
        own,
    )
    return updated.reshape(x.shape), own


def solution(mesh):
    return jax.shard_map(
        per_device,
        mesh=mesh,
        in_specs=(P(("grp", "gx"), None, None, None), P(), P(), P(), P(), P(), P(), P(), P()),
        out_specs=(P(("grp", "gx"), None, None, None), P(("grp", "gx"), None)),
        check_vma=False,
    )
```

```python
import functools
import math

import jax
import jax.numpy as jnp
from jax import lax
from jax.experimental import pallas as pl
from jax.experimental.pallas import tpu as pltpu
from jax.sharding import PartitionSpec as P

epsilon = 1e-05
MESH = pl.DeviceIdType.MESH
F32 = jnp.float32
BF16 = jnp.bfloat16
LANES = 128
MIB = 1024 * 1024
SLAB_LIMIT = 32 * MIB
SMALL_LIMIT = 12 * MIB
CONV_UNROLL = 8
SOFT_UNROLL = 1
STEP_ROWS = 256


def gelu(v):
    a = math.sqrt(2.0 / math.pi)
    return 0.5 * v * (1.0 + jnp.tanh(v * (a + (a * 0.044715) * (v * v))))


def slab_kernel(
    n, step_rows, x_ref, taps_hbm, aff_hbm, soft_hbm, p_out, g_out,
    taps_ref, aff_ref, soft_ref, pad, hid, prob, acc,
    load_sem, small_sem, store_sem, send_sem, recv_sem,
):
    planes, rows_y, rows_z, channels = x_ref.shape
    cells = rows_y * rows_z
    slices = aff_ref.shape[1]
    me = lax.axis_index("gx")
    inside = pl.ds(1, rows_y)
    has_left, has_right = me > 0, me < n - 1
    core, early = lax.rem(me, 2), max(planes - 2, 0)

    small = []
    for i, (src, dst) in enumerate(
        ((taps_hbm, taps_ref), (aff_hbm, aff_ref), (soft_hbm, soft_ref))
    ):
        copy = pltpu.make_async_copy(src, dst, small_sem.at[i])
        copy.start()
        small.append(copy)
    loads = []
    for j in range(planes):
        copy = pltpu.make_async_copy(x_ref.at[j], pad.at[j + 1, inside], load_sem.at[j])
        copy.start()
        loads.append(copy)

    barrier = pltpu.get_barrier_semaphore()

    @pl.when(has_left)
    def _():
        pl.semaphore_signal(barrier, inc=1, device_id={"gx": me - 1}, device_id_type=MESH)

    @pl.when(has_right)
    def _():
        pl.semaphore_signal(barrier, inc=1, device_id={"gx": me + 1}, device_id_type=MESH)

    pl.semaphore_wait(barrier, jnp.minimum(me, 1) + jnp.minimum(n - 1 - me, 1))

    up = pltpu.make_async_remote_copy(
        src_ref=x_ref.at[planes - 1], dst_ref=pad.at[0, inside],
        send_sem=send_sem.at[0], recv_sem=recv_sem.at[0],
        device_id={"gx": me + 1}, device_id_type=MESH,
    )
    down = pltpu.make_async_remote_copy(
        src_ref=x_ref.at[0], dst_ref=pad.at[planes + 1, inside],
        send_sem=send_sem.at[1], recv_sem=recv_sem.at[1],
        device_id={"gx": me - 1}, device_id_type=MESH,
    )

    @pl.when(has_right)
    def _():
        up.start()

    @pl.when(has_left)
    def _():
        down.start()

    for i in range(planes + 2):
        pad[i, 0] = jnp.zeros((rows_z, channels), BF16)
        pad[i, rows_y + 1] = jnp.zeros((rows_z, channels), BF16)

    @pl.when(jnp.logical_not(has_left))
    def _():
        pad[0, inside] = jnp.zeros((rows_y, rows_z, channels), BF16)

    @pl.when(jnp.logical_not(has_right))
    def _():
        pad[planes + 1, inside] = jnp.zeros((rows_y, rows_z, channels), BF16)

    acc[...] = jnp.zeros_like(acc)
    for copy in loads[:3] + small:
        copy.wait()

    row = lax.broadcasted_iota(jnp.int32, (rows_z, LANES), 0)
    soft = jnp.broadcast_to(soft_ref[...].astype(BF16), (LANES, channels))

    def plane(i, carry):
        @pl.when(i == min(1, planes - 1))
        def _():
            for copy in loads[3:]:
                copy.wait()

        @pl.when(jnp.logical_and(i == jnp.where(core == 0, planes - 1, early), has_left))
        def _():
            up.wait_recv()

        @pl.when(jnp.logical_and(i == jnp.where(core == 0, early, planes - 1), has_right))
        def _():
            down.wait_recv()

        p = jnp.where(i < planes - 2, i + 1, jnp.where((i == planes - 1) == (core == 0), 0, planes - 1))

        for ch in range(channels // LANES):
            cs = pl.ds(ch * LANES, LANES)
            taps = [
                jnp.broadcast_to(taps_ref[t : t + 1, cs], (rows_z, LANES)).astype(BF16)
                for t in range(27)
            ]

            def conv_row(y, carry):
                sums = [None, None, None]
                for a in range(3):
                    parts = [None, None, None]
                    for b in range(3):
                        v = pad[p + a, y + b, :, cs]
                        for c in range(3):
                            t = taps[9 * a + 3 * b + c] * v
                            parts[c] = t if parts[c] is None else parts[c] + t
                    for c in range(3):
                        sums[c] = parts[c] if sums[c] is None else sums[c] + parts[c]
                s0, s1, s2 = (t.astype(F32) for t in sums)
                total = (
                    s1
                    + jnp.where(row == 0, 0.0, pltpu.roll(s0, 1, 0))
                    + jnp.where(row == rows_z - 1, 0.0, pltpu.roll(s2, rows_z - 1, 0))
                )
                hid[pl.ds(pl.multiple_of(y * rows_z, rows_z), rows_z), cs] = gelu(
                    total
                ).astype(BF16)
                return carry

            lax.fori_loop(0, rows_y, conv_row, 0, unroll=CONV_UNROLL)

        def soft_step(j, carry):
            rs = pl.ds(pl.multiple_of(j * step_rows, step_rows), step_rows)
            h = hid[rs, :]
            logits = jnp.dot(h, aff_ref[...], preferred_element_type=F32)
            z = lax.dot_general(h, soft, (((1,), (1,)), ((), ())), preferred_element_type=F32)[:, :1]
            temp = 0.25 + jnp.maximum(z, 0.0) + jnp.log1p(jnp.exp(-jnp.abs(z)))
            top = jnp.max(logits, axis=-1, keepdims=True)
            e = jnp.exp((logits - top) * (1.0 / temp))
            prob[p, rs, :] = (e * (1.0 / jnp.sum(e, axis=-1, keepdims=True))).astype(BF16)
            return carry

        lax.fori_loop(0, cells // step_rows, soft_step, 0, unroll=SOFT_UNROLL)
        pltpu.make_async_copy(prob.at[p], p_out.at[p], store_sem.at[p]).start()
        contract = (((0,), (0,)), ((), ()))
        pk = prob[p]
        ones = jnp.ones((cells, LANES), BF16)
        acc[:, :channels] += lax.dot_general(pk, hid[...], contract, preferred_element_type=F32)
        acc[:, channels:] += lax.dot_general(pk, ones, contract, preferred_element_type=F32)
        return carry

    lax.fori_loop(0, planes, plane, 0)
    g_out[:, :channels] = acc[:, :channels].astype(BF16)
    mass = acc[:, channels:]
    high = mass.astype(BF16).astype(F32)
    lane = lax.broadcasted_iota(jnp.int32, (slices, LANES), 1)
    g_out[:, channels:] = jnp.where(lane < LANES // 2, high, mass - high).astype(BF16)
    for j in range(planes):
        pltpu.make_async_copy(prob.at[j], p_out.at[j], store_sem.at[j]).wait()

    @pl.when(has_right)
    def _():
        up.wait_send()

    @pl.when(has_left)
    def _():
        down.wait_send()


def slab(n, x, taps, aff, soft):
    planes, rows_y, rows_z, channels = x.shape
    slices = aff.shape[1]
    cells = rows_y * rows_z
    any_spec = pl.BlockSpec(memory_space=pl.ANY)
    vmem_spec = pl.BlockSpec(memory_space=pltpu.VMEM)
    dma = pltpu.SemaphoreType.DMA
    return pl.pallas_call(
        functools.partial(slab_kernel, n, min(STEP_ROWS, cells)),
        out_shape=(
            jax.ShapeDtypeStruct((planes, cells, slices), BF16),
            jax.ShapeDtypeStruct((slices, channels + LANES), BF16),
        ),
        in_specs=[pl.BlockSpec(memory_space=pltpu.HBM)] * 4,
        out_specs=(any_spec, vmem_spec),
        scratch_shapes=[
            pltpu.VMEM(taps.shape, F32),
            pltpu.VMEM(aff.shape, BF16),
            pltpu.VMEM(soft.shape, F32),
            pltpu.VMEM((planes + 2, rows_y + 2, rows_z, channels), BF16),
            pltpu.VMEM((cells, channels), BF16),
            pltpu.VMEM((planes, cells, slices), BF16),
            pltpu.VMEM((slices, channels + LANES), F32),
            dma((planes,)),
            dma((3,)),
            dma((planes,)),
            dma((2,)),
            dma((2,)),
        ],
        compiler_params=pltpu.CompilerParams(
            collective_id=1, has_side_effects=True, vmem_limit_bytes=SLAB_LIMIT
        ),
        name="slab",
    )(x, taps, aff, soft)


def exchange_kernel(
    n,
    g_ref,
    gain_hbm,
    wc_hbm,
    w1_hbm,
    w2_hbm,
    wf_hbm,
    own_ref,
    all_ref,
    gain_ref,
    wc,
    w1,
    w2,
    wf,
    pair_in,
    summed,
    ring_in,
    w_sem,
    s1,
    r1,
    s2,
    r2,
    s3,
    r3,
    s4,
    r4,
):
    me = lax.axis_index("gx")
    half = n // 2
    core = lax.rem(me, 2)
    chip = me // 2
    partner = me + 1 - 2 * core
    channels = wc.shape[0]

    def there(d):
        return 2 * lax.rem(chip + d, half) + core

    def origin(d):
        return lax.rem(chip + half - d, half)

    loads = []
    for i, (src, dst) in enumerate(
        ((wc_hbm, wc), (w1_hbm, w1), (w2_hbm, w2), (wf_hbm, wf), (gain_hbm, gain_ref))
    ):
        copy = pltpu.make_async_copy(src, dst, w_sem.at[i])
        copy.start()
        loads.append(copy)

    barrier = pltpu.get_barrier_semaphore()
    pl.semaphore_signal(barrier, inc=1, device_id={"gx": partner}, device_id_type=MESH)
    for d in range(1, half):
        pl.semaphore_signal(barrier, inc=1, device_id={"gx": there(d)}, device_id_type=MESH)
    pl.semaphore_wait(barrier, half)

    def remote(src, dst, ss, rs, to):
        return pltpu.make_async_remote_copy(
            src_ref=src, dst_ref=dst, send_sem=ss, recv_sem=rs,
            device_id={"gx": to}, device_id_type=MESH,
        )

    pair = []
    for d in range(half):
        k = lax.rem(chip + (d + 1) % half, half)
        copy = remote(g_ref.at[k, 1 - core], pair_in.at[k], s1.at[d], r1.at[d], partner)
        copy.start()
        pair.append(copy)
    sends = []
    for d in range(1, half):
        k = lax.rem(chip + d, half)
        pair[d - 1].wait_recv()
        summed[k] = (g_ref[k, core].astype(F32) + pair_in[k].astype(F32)).astype(BF16)
        copy = remote(summed.at[k], ring_in.at[d], s2.at[d], r2.at[d], there(d))
        copy.start()
        sends.append(copy)
    pair[half - 1].wait_recv()
    acc = g_ref[chip, core].astype(F32) + pair_in[chip].astype(F32)
    for d in range(1, half):
        sends[d - 1].wait_recv()
        acc = acc + ring_in[d].astype(F32)
    for copy in loads:
        copy.wait()

    mass = acc[:, channels : channels + 1] + acc[
        :, channels + LANES // 2 : channels + LANES // 2 + 1
    ]
    mean_hidden = acc[:, :channels] / (mass + epsilon)
    high = mean_hidden.astype(BF16)
    low = (mean_hidden - high.astype(F32)).astype(BF16)
    tokens = jnp.dot(high, wc[...], preferred_element_type=F32) + jnp.dot(
        low, wc[...], preferred_element_type=F32
    )
    center = jnp.mean(tokens, axis=-1, keepdims=True)
    spread = jnp.mean((tokens - center) ** 2, axis=-1, keepdims=True)
    normed = ((tokens - center) * (1.0 / jnp.sqrt(spread + epsilon)) * gain_ref[...]).astype(BF16)
    inner = gelu(jnp.dot(normed, w1[...], preferred_element_type=F32)).astype(BF16)
    own = (tokens + jnp.dot(inner, w2[...], preferred_element_type=F32)).astype(BF16)
    own_ref[...] = own
    all_ref[me] = jnp.dot(own, wf[...], preferred_element_type=F32).astype(BF16)

    out = []
    for d in range(1, half):
        copy = remote(all_ref.at[me], all_ref.at[me], s3.at[d], r3.at[d], there(d))
        copy.start()
        out.append(copy)
    first = remote(all_ref.at[me], all_ref.at[me], s4.at[0], r4.at[0], partner)
    first.start()
    relays = [first]
    for d in range(1, half):
        out[d - 1].wait_recv()
        block = 2 * origin(d) + core
        copy = remote(all_ref.at[block], all_ref.at[block], s4.at[d], r4.at[d], partner)
        copy.start()
        relays.append(copy)
    for copy in pair + sends + out:
        copy.wait_send()
    for copy in relays:
        copy.wait()


def exchange(n, g, gain, wc, w1, w2, wf):
    slices, width = g.shape
    channels = wc.shape[0]
    rows, half = slices // n, n // 2
    vmem_spec = pl.BlockSpec(memory_space=pltpu.VMEM)
    dma = pltpu.SemaphoreType.DMA
    return pl.pallas_call(
        functools.partial(exchange_kernel, n),
        out_shape=(
            jax.ShapeDtypeStruct((rows, channels), BF16),
            jax.ShapeDtypeStruct((n, rows, channels), BF16),
        ),
        in_specs=[vmem_spec] + [pl.BlockSpec(memory_space=pltpu.HBM)] * 5,
        out_specs=(vmem_spec, vmem_spec),
        scratch_shapes=[
            pltpu.VMEM(gain.shape, F32),
            pltpu.VMEM(wc.shape, BF16),
            pltpu.VMEM(w1.shape, BF16),
            pltpu.VMEM(w2.shape, BF16),
            pltpu.VMEM(wf.shape, BF16),
            pltpu.VMEM((half, rows, width), BF16),
            pltpu.VMEM((half, rows, width), BF16),
            pltpu.VMEM((half, rows, width), BF16),
            dma((5,)),
        ]
        + [dma((half,))] * 8,
        compiler_params=pltpu.CompilerParams(
            collective_id=0, has_side_effects=True, vmem_limit_bytes=SMALL_LIMIT
        ),
        name="exchange",
    )(g.reshape(half, 2, rows, width), gain, wc, w1, w2, wf)


def final_kernel(x_ref, p_ref, f_ref, own_ref, o_hbm, own_out, buf, sem):
    own_out[...] = own_ref[...]
    slots, block, _ = buf.shape
    steps = x_ref.shape[0] // block
    out = []
    for i in range(steps):
        rs = pl.ds(i * block, block)
        if i >= slots:
            out[i - slots].wait()
        buf[i % slots] = (
            x_ref[rs, :].astype(F32)
            + jnp.dot(p_ref[rs, :], f_ref[...], preferred_element_type=F32)
        ).astype(BF16)
        copy = pltpu.make_async_copy(buf.at[i % slots], o_hbm.at[rs, :], sem.at[i % slots])
        copy.start()
        out.append(copy)
    for copy in out[max(steps - slots, 0) :]:
        copy.wait()


def final(x, p, f, own):
    cells, channels = x.shape
    block = math.gcd(cells, 512)
    vmem_spec = pl.BlockSpec(memory_space=pltpu.VMEM)
    return pl.pallas_call(
        final_kernel,
        out_shape=(
            jax.ShapeDtypeStruct((cells, channels), BF16),
            jax.ShapeDtypeStruct(own.shape, BF16),
        ),
        in_specs=[vmem_spec] * 4,
        out_specs=(pl.BlockSpec(memory_space=pl.ANY), vmem_spec),
        scratch_shapes=[
            pltpu.VMEM((3, block, channels), BF16),
            pltpu.SemaphoreType.DMA((3,)),
        ],
        compiler_params=pltpu.CompilerParams(vmem_limit_bytes=SMALL_LIMIT),
        name="final",
    )(x, p, f, own)


def per_device(x, stencil, aff, softness, wc, gain, w1, w2, wf):
    planes, rows_y, rows_z, channels = x.shape
    n = lax.axis_size("gx")
    def held(v):
        return pltpu.with_memory_space_constraint(v, pltpu.HBM)

    probs, g = slab(n, held(x), held(stencil), held(aff), held(softness.reshape(1, -1)))
    own, folded = exchange(
        n, g, held(gain.reshape(1, -1)), held(wc), held(w1), held(w2), held(wf)
    )
    updated, own = final(
        x.reshape(-1, channels),
        probs.reshape(planes * rows_y * rows_z, -1),
        folded.reshape(-1, channels),
        own,
    )
    return updated.reshape(x.shape), own


def solution(mesh):
    return jax.shard_map(
        per_device,
        mesh=mesh,
        in_specs=(P(("grp", "gx"), None, None, None), P(), P(), P(), P(), P(), P(), P(), P()),
        out_specs=(P(("grp", "gx"), None, None, None), P(("grp", "gx"), None)),
        check_vma=False,
    )
```
